32 devices in a mesh: shard: 4 (over z), replica: 8 (over y, x, core).
Axes of the slice: x: 2, y: 2, z: 4, core: 2. Of those that a mesh axis runs over, the one named last changes fastest.
Arguments:
- momentum: bfloat16 [8, 4, 2048, 512], P('replica', None, 'shard'), may hold values from -6 to 6
- weight: bfloat16 [4, 2048, 512], P(None, 'shard', 'replica'), may hold values from -0.25 to 0.25
Outputs:
- new_weight: bfloat16 [4, 2048, 512], P(None, 'shard', 'replica')
- update: float32 [4, 2048, 512], P(None, 'shard', 'replica')
The draws below stay inside these ranges and needn't reach their ends.
All inputs are finite; a program needn't handle non-finite values.
Results may differ from the reference program's by a relative error of at most 0.0058.
Values may be sent and summed in bfloat16 or wider, within the bound.
No kernel may reach another device: no remote copies, remote signals or barrier semaphores. Data moves between devices by JAX's collectives and lax.ppermute only.
A program may use at most 64 MiB of HBM per device.

```python
import math
import jax
import jax.numpy as jnp
from jax import lax

D = 2048
FF = 512
ITERS = 2
MATS = 4
REPLICAS = 8


def level_of(own_key, dims, pieces, smallest, top_value):
    level = 1.0
    for axis_at, blocks in pieces:
        draws = jax.random.uniform(jax.random.fold_in(jax.random.fold_in(own_key, 6), axis_at), (blocks,), jnp.float32, smallest / len(pieces), top_value / len(pieces))
        level = level * jnp.repeat(jnp.exp(draws), dims[axis_at] // blocks).reshape((-1,) + (1,) * (len(dims) - 1 - axis_at))
    return level


def normal_values(stream_key, dims, deviation, bound, shards=(), held_as=jnp.bfloat16):
    array = deviation * jax.random.normal(stream_key, dims, jnp.float32)
    if shards:
        array = array * level_of(stream_key, dims, shards, -0.22, 0.18)
    return jnp.clip(array, -bound, bound).astype(held_as)


def setup_inputs(seed: int = 0) -> dict:
    arg_keys = jax.random.split(jax.random.key(seed), 3)
    momentum = normal_values(arg_keys[0], (REPLICAS, MATS, D, FF), 1.0, 6.0, ((0, 8), (2, 4)))
    weight = normal_values(arg_keys[1], (MATS, D, FF), FF ** -0.5, 0.25, ((1, 4), (2, 8)))
    return {"momentum": momentum, "weight": weight}


coef_a = 3.4445
coef_b = -4.775
coef_c = 2.0315
learn_rate = 0.02
decay_rate = 0.1
norm_eps = 1e-07

def newton(matrix):
    values = matrix.astype(jnp.float32)
    frob_norm = jnp.sqrt(jnp.sum(values * values))
    iterate = (values / (frob_norm + norm_eps)).astype(jnp.bfloat16)
    for step in range(ITERS):
        gram = lax.dot_general(iterate, iterate, (((0,), (0,)), ((), ())), preferred_element_type=jnp.float32).astype(jnp.bfloat16)
        gram_sq = jnp.dot(gram, gram, preferred_element_type=jnp.float32)
        poly = (coef_b * gram.astype(jnp.float32) + coef_c * gram_sq).astype(jnp.bfloat16)
        iterate = (coef_a * iterate.astype(jnp.float32) + jnp.dot(iterate, poly, preferred_element_type=jnp.float32)).astype(jnp.bfloat16)
    return iterate

def reference(momentum, weight):
    muon_scale = 0.2 * math.sqrt(max(D, FF))

    def add_replica(index, summed):
        ortho = lax.map(newton, momentum[index])
        return summed + muon_scale * ortho.astype(jnp.float32)
    summed = lax.fori_loop(0, REPLICAS, add_replica, jnp.zeros((MATS, D, FF), jnp.float32))
    update = summed / REPLICAS
    new_weight = (weight.astype(jnp.float32) * (1.0 - learn_rate * decay_rate) - learn_rate * update).astype(jnp.bfloat16)
    return (new_weight, update)
```

```python
import functools
import math

import jax
import jax.numpy as jnp
from jax import lax
from jax.experimental import pallas as pl
from jax.experimental.pallas import tpu as pltpu
from jax.sharding import PartitionSpec as P

coef_a = 3.4445
coef_b = -4.775
coef_c = 2.0315
learn_rate = 0.02
decay_rate = 0.1
norm_eps = 1e-07

LANE = 128
F32 = jnp.float32
BF16 = jnp.bfloat16

VMEM = pl.BlockSpec(memory_space=pltpu.VMEM)
SMEM = pl.BlockSpec(memory_space=pltpu.SMEM)


def call(body, out_shape, n_in, n_smem=0, flops=0, bytes_accessed=0, in_specs=None, **kw):
    return pl.pallas_call(
        body,
        out_shape=out_shape,
        in_specs=in_specs or [SMEM] * n_smem + [VMEM] * n_in,
        out_specs=jax.tree.map(lambda _: VMEM, out_shape),
        cost_estimate=pl.CostEstimate(
            flops=flops, bytes_accessed=bytes_accessed, transcendentals=0
        ),
        **kw,
    )


def dot(a, b):
    return jnp.dot(a, b, preferred_element_type=F32)


def block_pairs(width):
    nb = width // LANE
    return [(i, j) for i in range(nb) for j in range(i + 1, nb)]


def packed_rows(width):
    return width * width // 2 // LANE + 16


def grid_index():
    row = lax.broadcasted_iota(jnp.int32, (LANE, LANE), 0)
    col = lax.broadcasted_iota(jnp.int32, (LANE, LANE), 1)
    return row, col


def two_terms(diagonal):
    high = diagonal.astype(BF16).astype(F32)
    return jnp.concatenate([high, diagonal - high], axis=0).astype(BF16)


def gram_body(x_ref, packed_ref, xt_ref):
    x = x_ref[...]
    width = x.shape[1]
    nb = width // LANE
    xt = x.T
    xt_ref[...] = xt
    half = max(width // 2, LANE)
    strips = [dot(xt[k : k + half], x[:, k:]) for k in range(0, width, half)]

    def block(i, j):
        k = i * LANE // half
        r = i * LANE - k * half
        c = j * LANE - k * half
        return strips[k][r : r + LANE, c : c + LANE]

    at = 0
    for i, j in block_pairs(width):
        packed_ref[at : at + LANE, :] = block(i, j).astype(BF16)
        at += LANE
    row, col = grid_index()
    for i in range(0, nb, 2):
        packed_ref[at : at + LANE, :] = jnp.where(
            row <= col, block(i, i), block(i + 1, i + 1)
        ).astype(BF16)
        at += LANE
    rows = [
        jnp.sum(jnp.where(row == col, block(i, i), 0.0), axis=0, keepdims=True) for i in range(nb)
    ]
    rows.append(jnp.zeros((8 - nb, LANE), F32))
    packed_ref[at : at + 16, :] = two_terms(jnp.concatenate(rows, axis=0))


def gram(momentum, m):
    rows, width = momentum.shape[1:]
    return call(
        gram_body,
        (
            jax.ShapeDtypeStruct((packed_rows(width), LANE), BF16),
            jax.ShapeDtypeStruct((width, rows), BF16),
        ),
        1,
        flops=2 * rows * width * width,
        bytes_accessed=2 * rows * width,
        in_specs=[
            pl.BlockSpec((pl.Squeezed(), rows, width), lambda i: (m, 0, 0)),
        ],
        grid=(1,),
    )(momentum)


def add_body(a_ref, b_ref, out_ref):
    body = a_ref.shape[0] - 16
    out_ref[:body, :] = (a_ref[:body, :].astype(F32) + b_ref[:body, :].astype(F32)).astype(BF16)
    tail = a_ref[body:, :].astype(F32) + b_ref[body:, :].astype(F32)
    out_ref[body:, :] = two_terms(tail[:8] + tail[8:])


def add_packed(a, b):
    return call(
        add_body,
        jax.ShapeDtypeStruct(a.shape, a.dtype),
        2,
        flops=a.size,
        bytes_accessed=6 * a.size,
    )(a, b)


def newton_body(place_ref, own_ref, got_ref, xt_ref, keep_ref, send_ref, g_ref):
    width = xt_ref.shape[0]
    nb = width // LANE
    take = place_ref[0] == 1
    core = place_ref[1]
    body = own_ref.shape[0] - 16

    def pick(start, count):
        return jnp.where(take, got_ref[start : start + count, :], own_ref[start : start + count, :])

    tail = pick(body, 16).astype(F32)
    diagonal = tail[:8] + tail[8:]
    norm = jnp.sqrt(jnp.sum(diagonal, keepdims=True))
    scale = 1.0 / (norm + norm_eps)
    square = scale * scale
    at = 0
    for i, j in block_pairs(width):
        blk = pick(at, LANE)
        g_ref[i * LANE : (i + 1) * LANE, j * LANE : (j + 1) * LANE] = blk
        g_ref[j * LANE : (j + 1) * LANE, i * LANE : (i + 1) * LANE] = blk.T
        at += LANE
    row, col = grid_index()
    for i in range(0, nb, 2):
        blk = pick(at, LANE).astype(F32)
        flip = blk.T
        at += LANE
        even = jnp.where(row <= col, blk, flip)
        odd = jnp.where(row > col, blk, flip)
        odd = jnp.where(row == col, jnp.broadcast_to(diagonal[i + 1 : i + 2], (LANE, LANE)), odd)
        for k, value in ((i, even), (i + 1, odd)):
            g_ref[k * LANE : (k + 1) * LANE, k * LANE : (k + 1) * LANE] = value.astype(BF16)
    g = g_ref[...]
    poly0 = ((coef_b * square) * g.astype(F32) + (coef_c * square * square) * dot(g, g)).astype(
        BF16
    )
    turned = square * (coef_a * g.astype(F32) + dot(g, poly0))
    gram1 = (coef_a * turned + dot(turned.astype(BF16), poly0)).astype(BF16)
    poly1 = (coef_b * gram1.astype(F32) + coef_c * dot(gram1, gram1)).astype(BF16)
    xt = xt_ref[...]
    first = scale * (coef_a * xt.astype(F32) + dot(poly0, xt))
    ortho = coef_a * first + dot(poly1, first.astype(BF16))
    piece = keep_ref.shape[1]
    for k in range(keep_ref.shape[0]):
        zero = ortho[2 * k * piece : (2 * k + 1) * piece]
        one = ortho[(2 * k + 1) * piece : (2 * k + 2) * piece]
        keep_ref[k] = jnp.where(core == 0, zero, one).astype(BF16)
        send_ref[k] = jnp.where(core == 0, one, zero).astype(BF16)


def newton(place, own, got, xt, replica_count):
    width, rows = xt.shape
    half = jax.ShapeDtypeStruct((replica_count // 2, width // replica_count, rows), BF16)
    return call(
        newton_body,
        (half, half),
        3,
        n_smem=1,
        flops=2 * width * width * (4 * width + 2 * rows),
        bytes_accessed=2 * own.size * 2 + 4 * xt.size,
        scratch_shapes=[pltpu.VMEM((width, width), BF16)],
    )(place, own, got, xt)


def pair_body(place_ref, keep_ref, got_ref, *out_refs):
    chip = place_ref[2]
    for d, out_ref in enumerate(out_refs):
        at = chip ^ d
        out_ref[...] = (keep_ref[at].astype(F32) + got_ref[at].astype(F32)).astype(out_ref.dtype)


def pair_sum(place, keep, got):
    chips = keep.shape[0]
    return call(
        pair_body,
        tuple(
            jax.ShapeDtypeStruct(keep.shape[1:], F32 if d == 0 else BF16) for d in range(chips)
        ),
        2,
        n_smem=1,
        flops=keep.size,
        bytes_accessed=6 * keep.size,
    )(place, keep, got)


def final_body(scale, chips, weight_ref, *refs):
    update_ref, new_ref = refs[-2:]
    for m in range(weight_ref.shape[0]):
        parts = refs[m * chips : (m + 1) * chips]
        total = parts[0][...]
        for part in parts[1:]:
            total = total + part[...].astype(F32)
        update = scale * total
        update_ref[m] = update
        new_ref[m] = (
            weight_ref[m].astype(F32) * (1.0 - learn_rate * decay_rate) - learn_rate * update
        ).astype(BF16)


def local(momentum, weight):
    n = lax.axis_size("shard")
    replica_count = lax.axis_size("replica")
    chips = replica_count // 2
    momentum = momentum[0]
    mats, rows, width = momentum.shape
    muon_scale = 0.2 * math.sqrt(max(n * rows, width))
    z = lax.axis_index("shard")
    r = lax.axis_index("replica")
    outer = ((z < n // 2 - 1) | (z > n // 2)).astype(jnp.int32)
    place = jnp.stack([outer, r % 2, r // 2]).astype(jnp.int32)

    packed, flipped = zip(*[gram(momentum, m) for m in range(mats)])
    packed = list(packed)
    for m in range(mats):
        for h in range(n // 2 - 1):
            got = lax.ppermute(packed[m], "shard", [(h, h + 1), (n - 1 - h, n - 2 - h)])
            packed[m] = add_packed(packed[m], got)
    parts = []
    for m in range(mats):
        lo, hi = n // 2 - 1, n // 2
        total = add_packed(packed[m], lax.ppermute(packed[m], "shard", [(lo, hi), (hi, lo)]))
        got = total
        for h in range(lo, 0, -1):
            back = lax.ppermute(got, "shard", [(h, h - 1), (n - 1 - h, n - h)])
            got = back if h == lo else jnp.where((z >= h) & (z <= n - 1 - h), got, back)
        keep, send = newton(place, total, got, flipped[m], replica_count)
        swapped = lax.ppermute(send, "replica", [(i, i ^ 1) for i in range(replica_count)])
        sums = pair_sum(place, keep, swapped)
        parts.append(sums[0])
        for d in range(1, chips):
            parts.append(
                lax.ppermute(
                    sums[d], "replica", [(i, i ^ (2 * d)) for i in range(replica_count)]
                )
            )
    weight = jnp.swapaxes(weight, 1, 2)
    update, new_weight = call(
        functools.partial(final_body, muon_scale / replica_count, chips),
        (
            jax.ShapeDtypeStruct(weight.shape, F32),
            jax.ShapeDtypeStruct(weight.shape, BF16),
        ),
        1 + len(parts),
        flops=weight.size * replica_count,
        bytes_accessed=weight.size * replica_count,
    )(weight, *parts)
    return (jnp.swapaxes(new_weight, 1, 2), jnp.swapaxes(update, 1, 2))


def solution(mesh):
    in_specs = (P("replica", None, "shard", None), P(None, "shard", "replica"))
    out_specs = (P(None, "shard", "replica"), P(None, "shard", "replica"))
    return jax.shard_map(local, mesh=mesh, in_specs=in_specs, out_specs=out_specs, check_vma=False)
```

```python
import functools
import math

import jax
import jax.numpy as jnp
from jax import lax
from jax.experimental import pallas as pl
from jax.experimental.pallas import tpu as pltpu
from jax.sharding import PartitionSpec as P


coef_a = 3.4445
coef_b = -4.775
coef_c = 2.0315
learn_rate = 0.02
decay_rate = 0.1
norm_eps = 1e-07

LANE = 128
RESIDENT_BYTES = 2**21
F32 = jnp.float32
BF16 = jnp.bfloat16

VMEM = pltpu.VMEM
HBM = pltpu.HBM


def call(
    resident, body, out_shape, spaces, flops=0, bytes_accessed=0, in_hbm=False, **kw
):
    hold = resident and not in_hbm
    fn = pl.pallas_call(
        body,
        out_shape=jax.tree.map(lambda s: VMEM(s.shape, s.dtype), out_shape) if hold else out_shape,
        in_specs=[pl.BlockSpec(memory_space=space) for space in spaces],
        out_specs=jax.tree.map(lambda _: pl.BlockSpec(memory_space=VMEM), out_shape),
        cost_estimate=pl.CostEstimate(
            flops=flops, bytes_accessed=bytes_accessed, transcendentals=0
        ),
        **kw,
    )
    if not resident:
        return fn
    return lambda *args: fn(
        *[pltpu.with_memory_space_constraint(a, space) for a, space in zip(args, spaces)]
    )


def dot(a, b):
    return jnp.dot(a, b, preferred_element_type=F32)


def block_pairs(width):
    nb = width // LANE
    return [(i, j) for i in range(nb) for j in range(i + 1, nb)]


def packed_rows(width):
    return width * width // 2 // LANE + 16


def grid_index():
    row = lax.broadcasted_iota(jnp.int32, (LANE, LANE), 0)
    col = lax.broadcasted_iota(jnp.int32, (LANE, LANE), 1)
    return row, col


def two_terms(diagonal):
    high = diagonal.astype(BF16).astype(F32)
    return jnp.concatenate([high, diagonal - high], axis=0).astype(BF16)


def gram_body(mats, momentum_ref, *refs):
    count = len(mats)
    packed_refs, x_ref, sems = refs[:count], refs[count], refs[count + 1]
    copies = [
        pltpu.make_async_copy(momentum_ref.at[m], x_ref.at[k], sems.at[k])
        for k, m in enumerate(mats)
    ]
    for copy in copies:
        copy.start()
    for k, copy in enumerate(copies):
        copy.wait()
        pack_gram(x_ref[k], packed_refs[k])


def pack_gram(x, packed_ref):
    width = x.shape[1]
    nb = width // LANE
    xt = x.T
    half = max(width // 2, LANE)
    strips = [dot(xt[k : k + half], x[:, k:]) for k in range(0, width, half)]

    def block(i, j):
        k = i * LANE // half
        r = i * LANE - k * half
        c = j * LANE - k * half
        return strips[k][r : r + LANE, c : c + LANE]

    at = 0
    for i, j in block_pairs(width):
        packed_ref[at : at + LANE, :] = block(i, j).astype(BF16)
        at += LANE
    row, col = grid_index()
    for i in range(0, nb, 2):
        packed_ref[at : at + LANE, :] = jnp.where(
            row <= col, block(i, i), block(i + 1, i + 1)
        ).astype(BF16)
        at += LANE
    rows = [
        jnp.sum(jnp.where(row == col, block(i, i), 0.0), axis=0, keepdims=True) for i in range(nb)
    ]
    rows.append(jnp.zeros((8 - nb, LANE), F32))
    packed_ref[at : at + 16, :] = two_terms(jnp.concatenate(rows, axis=0))


def gram(resident, momentum, mats):
    rows, width = momentum.shape[1:]
    count = len(mats)
    shape = jax.ShapeDtypeStruct((packed_rows(width), LANE), BF16)
    return call(
        resident,
        functools.partial(gram_body, mats),
        (shape,) * count,
        (HBM,),
        flops=2 * count * rows * width * width,
        bytes_accessed=2 * count * rows * width,
        scratch_shapes=[
            pltpu.VMEM((count, rows, width), BF16),
            pltpu.SemaphoreType.DMA((count,)),
        ],
    )(momentum)


def add_body(a_ref, b_ref, out_ref):
    body = a_ref.shape[0] - 16
    out_ref[:body, :] = (a_ref[:body, :].astype(F32) + b_ref[:body, :].astype(F32)).astype(BF16)
    tail = a_ref[body:, :].astype(F32) + b_ref[body:, :].astype(F32)
    out_ref[body:, :] = two_terms(tail[:8] + tail[8:])


def add_packed(resident, a, b):
    return call(
        resident,
        add_body,
        jax.ShapeDtypeStruct(a.shape, a.dtype),
        (VMEM, VMEM),
        flops=a.size,
        bytes_accessed=6 * a.size,
    )(a, b)


def newton_body(m, own_ref, got_ref, momentum_ref, keep_ref, send_ref, g_ref, x_ref, sem):
    copy = pltpu.make_async_copy(momentum_ref.at[m], x_ref, sem)
    copy.start()
    width = x_ref.shape[1]
    nb = width // LANE
    z = lax.axis_index("shard")
    n = lax.axis_size("shard")
    take = (z < n // 2 - 1) | (z > n // 2)
    core = lax.axis_index("replica") % 2
    body = own_ref.shape[0] - 16

    def pick(start, count):
        return jnp.where(take, got_ref[start : start + count, :], own_ref[start : start + count, :])

    tail = pick(body, 16).astype(F32)
    diagonal = tail[:8] + tail[8:]
    norm = jnp.sqrt(jnp.sum(diagonal, keepdims=True))
    scale = 1.0 / (norm + norm_eps)
    square = scale * scale
    at = 0
    for i, j in block_pairs(width):
        blk = pick(at, LANE)
        g_ref[i * LANE : (i + 1) * LANE, j * LANE : (j + 1) * LANE] = blk
        g_ref[j * LANE : (j + 1) * LANE, i * LANE : (i + 1) * LANE] = blk.T
        at += LANE
    row, col = grid_index()
    for i in range(0, nb, 2):
        blk = pick(at, LANE).astype(F32)
        flip = blk.T
        at += LANE
        even = jnp.where(row <= col, blk, flip)
        odd = jnp.where(row > col, blk, flip)
        odd = jnp.where(row == col, jnp.broadcast_to(diagonal[i + 1 : i + 2], (LANE, LANE)), odd)
        for k, value in ((i, even), (i + 1, odd)):
            g_ref[k * LANE : (k + 1) * LANE, k * LANE : (k + 1) * LANE] = value.astype(BF16)
    g = g_ref[...]
    poly0 = ((coef_b * square) * g.astype(F32) + (coef_c * square * square) * dot(g, g)).astype(
        BF16
    )
    turned = square * (coef_a * g.astype(F32) + dot(g, poly0))
    gram1 = (coef_a * turned + dot(turned.astype(BF16), poly0)).astype(BF16)
    poly1 = (coef_b * gram1.astype(F32) + coef_c * dot(gram1, gram1)).astype(BF16)
    copy.wait()
    xt = x_ref[...].T
    first = scale * (coef_a * xt.astype(F32) + dot(poly0, xt))
    ortho = coef_a * first + dot(poly1, first.astype(BF16))
    piece = keep_ref.shape[1]
    for k in range(keep_ref.shape[0]):
        zero = ortho[2 * k * piece : (2 * k + 1) * piece]
        one = ortho[(2 * k + 1) * piece : (2 * k + 2) * piece]
        keep_ref[k] = jnp.where(core == 0, zero, one).astype(BF16)
        send_ref[k] = jnp.where(core == 0, one, zero).astype(BF16)


def newton(resident, own, got, momentum, m, replica_count):
    rows, width = momentum.shape[1:]
    half = jax.ShapeDtypeStruct((replica_count // 2, width // replica_count, rows), BF16)
    return call(
        resident,
        functools.partial(newton_body, m),
        (half, half),
        (VMEM, VMEM, HBM),
        flops=2 * width * width * (4 * width + 2 * rows),
        bytes_accessed=2 * own.size * 2 + 4 * rows * width,
        scratch_shapes=[
            pltpu.VMEM((width, width), BF16),
            pltpu.VMEM((rows, width), BF16),
            pltpu.SemaphoreType.DMA(()),
        ],
    )(own, got, momentum)


def pair_body(count, *refs):
    chip = lax.axis_index("replica") // 2
    keep_refs, got_refs, out_refs = refs[:count], refs[count : 2 * count], refs[2 * count :]
    for d, out_ref in enumerate(out_refs):
        at = chip ^ d
        for k in range(count):
            out_ref[k] = (
                keep_refs[k][at].astype(F32) + got_refs[k][at].astype(F32)
            ).astype(out_ref.dtype)


def pair_sum(resident, keep, got):
    count = len(keep)
    chips = keep[0].shape[0]
    shape = (count,) + keep[0].shape[1:]
    return call(
        resident,
        functools.partial(pair_body, count),
        tuple(jax.ShapeDtypeStruct(shape, F32 if d == 0 else BF16) for d in range(chips)),
        (VMEM,) * (2 * count),
        flops=count * keep[0].size,
        bytes_accessed=6 * count * keep[0].size,
    )(*keep, *got)


def final_body(scale, counts, chips, weight_ref, *refs):
    update_ref, new_ref = refs[-2:]
    m = 0
    for group, count in enumerate(counts):
        parts = refs[group * chips : (group + 1) * chips]
        for k in range(count):
            total = parts[0][k]
            for part in parts[1:]:
                total = total + part[k].astype(F32)
            update = scale * total
            update_ref[m] = update
            new_ref[m] = (
                weight_ref[m].astype(F32) * (1.0 - learn_rate * decay_rate) - learn_rate * update
            ).astype(BF16)
            m += 1


def groups_of(mats):
    early = list(range(max(mats - 2, 0)))
    return ([early] if early else []) + [[m] for m in range(len(early), mats)]


def local(momentum, weight):
    n = lax.axis_size("shard")
    replica_count = lax.axis_size("replica")
    chips = replica_count // 2
    momentum = momentum[0]
    mats, rows, width = momentum.shape
    resident = mats * packed_rows(width) * LANE * 2 <= RESIDENT_BYTES
    muon_scale = 0.2 * math.sqrt(max(n * rows, width))
    z = lax.axis_index("shard")
    lo, hi = n // 2 - 1, n // 2

    def swap(value, bits):
        return lax.ppermute(value, "replica", [(i, i ^ bits) for i in range(replica_count)])

    packed = []
    for part in ([0], list(range(1, mats))):
        packed.extend(gram(resident, momentum, part))
    for m in range(mats):
        for h in range(lo):
            got = lax.ppermute(packed[m], "shard", [(h, h + 1), (n - 1 - h, n - 2 - h)])
            packed[m] = add_packed(resident, packed[m], got)
    keeps, sends = [], []
    for m in range(mats):
        got = lax.ppermute(packed[m], "shard", [(lo, hi), (hi, lo)])
        total = add_packed(resident, packed[m], got)
        got = total
        for h in range(lo, 0, -1):
            back = lax.ppermute(got, "shard", [(h, h - 1), (n - 1 - h, n - h)])
            got = back if h == lo else jnp.where((z >= h) & (z <= n - 1 - h), got, back)
        keep, send = newton(
            resident, total, got, momentum, m, replica_count
        )
        sends.append(swap(send, 1))
        keeps.append(keep)
    parts = []
    groups = groups_of(mats)
    for group in groups:
        sums = pair_sum(resident, [keeps[m] for m in group], [sends[m] for m in group])
        parts.append(sums[0])
        for d in range(1, chips):
            parts.append(swap(sums[d], 2 * d))
    weight = jnp.swapaxes(weight, 1, 2)
    update, new_weight = call(
        resident,
        functools.partial(final_body, muon_scale / replica_count, [len(g) for g in groups], chips),
        (
            jax.ShapeDtypeStruct(weight.shape, F32),
            jax.ShapeDtypeStruct(weight.shape, BF16),
        ),
        (VMEM,) * (1 + len(parts)),
        flops=weight.size * replica_count,
        bytes_accessed=weight.size * replica_count,
        in_hbm=True,
    )(weight, *parts)
    return (jnp.swapaxes(new_weight, 1, 2), jnp.swapaxes(update, 1, 2))


def solution(mesh):
    in_specs = (P("replica", None, "shard", None), P(None, "shard", "replica"))
    out_specs = (P(None, "shard", "replica"), P(None, "shard", "replica"))
    return jax.shard_map(local, mesh=mesh, in_specs=in_specs, out_specs=out_specs, check_vma=False)
```
